256 devices in a mesh: pipe: 4 (over z_hi, core), expert: 64 (over x, z_lo, y).
Axes of the slice: x: 4, y: 4, z: 8 (z_hi: 2, z_lo: 4; z = z_hi * 4 + z_lo), core: 2. Of those that a mesh axis runs over, the one named last changes fastest.
Arguments:
- tokens: bfloat16 [4, 8192, 3584], P('pipe', 'expert'), may hold values from -6 to 6
- expert_ids: int32 [4, 8192, 4], P('pipe', 'expert'), may hold values from 0 to 63, all different within a row; in each aligned block of 128 rows (0 to 127, 128 to 255, ..., all dimensions but the last counted through in order) at most 14 rows name the same one
- up_weight: bfloat16 [4, 64, 3584, 512], P('pipe', 'expert'), may hold values from -0.1875 to 0.1875
- up_grad: bfloat16 [4, 64, 64, 14, 1024], P('pipe', 'expert'), may hold values from -1.1953125 to 1.1953125
Outputs:
- token_grad: bfloat16 [4, 8192, 3584], P('pipe', 'expert')
- weight_grad: bfloat16 [4, 64, 3584, 512], P('pipe', 'expert')
The draws below stay inside these ranges and needn't reach their ends.
Inputs may be any that keep to these rules, and one draw needn't show every extreme that they name: `expert_ids`: A token's 4 experts are distinct. Among the 128 tokens of one device no expert is named by more than 14 tokens, and on some device one expert is named by exactly 14.
All inputs are finite; a program needn't handle non-finite values.
Results may differ from the reference program's by a relative error of at most 0.0051.
Values may be sent and summed in bfloat16 or wider, within the bound.
No kernel may reach another device: no remote copies, remote signals or barrier semaphores. Data moves between devices by JAX's collectives and lax.ppermute only.
A program may use at most 128 MiB of HBM per device.

```python
import math
import jax
import jax.numpy as jnp
import numpy as np
from jax import lax

D = 3584
FF = 1024
TOP = 4
TOK_DEV = 128
SECTIONS = 4
EXPERTS = 64
TOKENS = 8192
FFH = 512
MOST = 14


def block_levels(rng, shape, shards, low, largest):
    def one(axis_at, parts):
        heights = jax.random.uniform(jax.random.fold_in(jax.random.fold_in(rng, 6), axis_at), (parts,), jnp.float32, low / len(shards), largest / len(shards))
        return jnp.repeat(jnp.exp(heights), shape[axis_at] // parts).reshape((-1,) + (1,) * (len(shape) - axis_at - 1))

    gain = one(*shards[0])
    for cut in shards[1:]:
        gain = gain * one(*cut)
    return gain


def shared_out(stream_key, own, number, rows, number_of, top, most, slope):
    ranking = jax.random.permutation(stream_key, number_of)
    heavy_load, ordinary = load_shares(number_of, rows * top, most, slope, True), load_shares(number_of, rows * top, most, slope, False)
    places = jnp.arange(number_of)

    def named(lengths, turn):
        used = int((lengths > 0).sum())
        fixed = max(1, used // 4)
        passed = fixed + (places - fixed + turn * (used - fixed)) % max(1, number_of - fixed)
        return jnp.zeros((number_of,), jnp.int32).at[ranking[jnp.where(places < fixed, places, passed)]].set(jnp.asarray(lengths, jnp.int32))

    lengths = jnp.where(number % 4 == 0, named(heavy_load, number // 4), named(ordinary, number - number // 4 - 1))
    mixed = jax.random.permutation(jax.random.fold_in(own, 3), number_of)
    giver, sink = mixed[0:number_of // 2 * 2:2], mixed[1:number_of // 2 * 2:2]
    room = jnp.minimum(lengths[giver] - 1, most - lengths[sink]) // 2
    room = jnp.where((giver == ranking[0]) | (sink == ranking[0]) | (lengths[sink] == 0), 0, jnp.maximum(room, 0))
    passed = jax.random.randint(jax.random.fold_in(own, 4), (number_of // 2,), 0, 1 << 20) % (room + 1)
    lengths = lengths.at[giver].add(-passed).at[sink].add(passed)
    labels = jnp.searchsorted(jnp.cumsum(lengths), jnp.arange(rows * top), side="right").astype(jnp.int32)
    listing = labels.reshape(top, rows).T
    listing = listing[jax.random.permutation(jax.random.fold_in(own, 1), rows)]
    turn = jax.random.randint(jax.random.fold_in(own, 2), (rows, 1), 0, top)
    return jnp.take_along_axis(listing, (jnp.arange(top)[None, :] + turn) % top, axis=1)


def load_shares(amount, total, bound, lean, full):
    weights = [(1 << 20) // math.isqrt(rank ** lean) + 1 for rank in range(1, amount + 1)]
    largest = bound if full else min(bound, max(-(-total // amount), total * weights[0] // sum(weights)))
    least = 1 if total - largest >= amount - 1 else 0
    holding, surplus = [largest] + [least] * (amount - 1), total - largest - least * (amount - 1)
    while surplus > 0:
        free = [i for i in range(1, amount) if holding[i] < largest] or [i for i in range(1, amount) if holding[i] < bound]
        whole, remaining = sum([weights[i] for i in free]), surplus
        for i in free:
            extra = min(bound - holding[i], max(1, remaining * weights[i] // whole), surplus)
            holding[i] = holding[i] + extra
            surplus = surplus - extra
    return np.array(holding)


def bell_draw(rng, extent, width, reach, shards=(), kind=jnp.bfloat16):
    level = block_levels(rng, extent, shards, -0.22, 0.18) if shards else 1.0
    values = jax.random.normal(rng, extent, jnp.float32) * width * level
    return jnp.minimum(jnp.maximum(values, -reach), reach).astype(kind)


def setup_inputs(seed: int = 0) -> dict:
    key_list = jax.random.split(jax.random.key(seed), 5)
    tokens = bell_draw(key_list[0], (SECTIONS, TOKENS, D), 1.0, 6.0, ((0, 4), (1, 64)))
    expert_ids_keys = jax.random.split(jax.random.fold_in(key_list[1], 1), SECTIONS * TOKENS // TOK_DEV)
    expert_ids_turns = jax.random.permutation(jax.random.fold_in(key_list[1], 3), SECTIONS * TOKENS // TOK_DEV)
    expert_ids = jax.vmap(lambda own, number: shared_out(jax.random.fold_in(key_list[1], 2), own, number, TOK_DEV, EXPERTS, TOP, MOST, 2))(expert_ids_keys, expert_ids_turns).reshape((SECTIONS, TOKENS, TOP))
    up_weight = bell_draw(key_list[2], (SECTIONS, EXPERTS, D, FFH), FF ** -0.5, 0.1875, ((0, 4), (1, 64)))
    up_grad = bell_draw(key_list[3], (SECTIONS, EXPERTS, EXPERTS, MOST, FF), 0.2, 1.1953125, ((0, 4), (1, 64)))
    return dict(tokens=tokens, expert_ids=expert_ids, up_weight=up_weight, up_grad=up_grad)


def reference(tokens, expert_ids, up_weight, up_grad):
    section_count = SECTIONS
    source_count = EXPERTS
    token_blocks = tokens.reshape(section_count, source_count, TOK_DEV, D)
    id_blocks = expert_ids.reshape(section_count, source_count, TOK_DEV, TOP)
    expert_lane = jnp.arange(EXPERTS, dtype=jnp.int32)
    named_count = jnp.sum((id_blocks[..., None] == expert_lane).astype(jnp.int32), axis=3)
    slot_before = jnp.cumsum(named_count, axis=2) - named_count
    slot_index = jnp.arange(MOST, dtype=jnp.int32)
    matches = (named_count[..., None] == 1) & (slot_before[..., None] == slot_index)
    token_lane = jnp.arange(TOK_DEV, dtype=jnp.int32)
    source_token = jnp.sum(matches.astype(jnp.int32) * token_lane[None, None, :, None, None], axis=2)
    slot_live = jnp.any(matches, axis=2)

    def per_expert(expert):
        partials = []
        row_list = []
        for section in range(section_count):
            lower = min(section, section_count - 1 - section)
            upper = section_count - 1 - lower
            full_weight = jnp.concatenate([up_weight[lower, expert], up_weight[upper, expert]], axis=1)
            picks = source_token[section, :, expert, :]
            arrived = jnp.take_along_axis(token_blocks[section], picks[:, :, None], axis=1)
            arrived = jnp.where(slot_live[section, :, expert, :][:, :, None], arrived, jnp.zeros_like(arrived))
            grad_rows = up_grad[section, expert]
            partial_value = jnp.einsum("sjd,sjf->df", arrived.astype(jnp.float32), grad_rows.astype(jnp.float32)).astype(jnp.bfloat16)
            row_grad = jnp.einsum("sjf,df->sjd", grad_rows.astype(jnp.float32), full_weight.astype(jnp.float32)).astype(jnp.bfloat16)
            partials.append(partial_value)
            row_list.append(row_grad)
        weight_list = []
        for section in range(section_count):
            side = 0 if section < section_count // 2 else 1
            mirror = section_count - 1 - section
            summed = partials[section][:, side * FFH:(side + 1) * FFH].astype(jnp.float32) + partials[mirror][:, side * FFH:(side + 1) * FFH].astype(jnp.float32)
            weight_list.append(summed.astype(jnp.bfloat16))
        return jnp.stack(weight_list), jnp.stack(row_list)

    weight_all, rows_all = lax.map(per_expert, jnp.arange(EXPERTS, dtype=jnp.int32))
    weight_grad = jnp.transpose(weight_all, (1, 0, 2, 3))
    slot_of = jnp.take_along_axis(slot_before, id_blocks, axis=3)
    source_lane = jnp.arange(source_count, dtype=jnp.int32)[:, None, None]

    def per_section(section):
        rows_section = rows_all[:, section]
        picked = rows_section[id_blocks[section], source_lane, slot_of[section]]
        return jnp.sum(picked.astype(jnp.float32), axis=2).astype(jnp.bfloat16)

    token_grad = lax.map(per_section, jnp.arange(section_count, dtype=jnp.int32)).reshape(section_count, TOKENS, D)
    return token_grad, weight_grad
```

```python
import jax
import jax.numpy as jnp
from jax import lax
from jax.sharding import Mesh, PartitionSpec as P

HI, CORE, X, LO, Y = "hi", "core", "x", "lo", "y"
AXES = (HI, CORE, X, LO, Y)


def mirror_pairs(sizes):
    n_hi, n_core, n_x, n_lo, n_y = sizes
    block = n_x * n_lo * n_y
    pairs = []
    for section in range(n_hi * n_core):
        for place in range(block):
            pairs.append((section * block + place, (n_hi * n_core - 1 - section) * block + place))
    return pairs


def mirror_rings(sizes):
    n_hi, n_core, n_x, n_lo, n_y = sizes
    return [
        [(hi * n_core + (core ^ hi)) * n_lo + lo for hi in range(n_hi) for lo in range(n_lo)]
        for core in range(n_core)
    ]


def dot(a, b, dims):
    return lax.dot_general(a, b, (dims, ((), ())), preferred_element_type=jnp.float32)


def on_device(sizes, tokens, expert_ids, up_weight, up_grad):
    n_hi, n_core, n_x, n_lo, n_y = sizes
    token_rows = tokens[0]
    width = token_rows.shape[1]
    count = token_rows.shape[0]
    weight = up_weight[0, 0]
    half = weight.shape[1]
    sources, most = up_grad.shape[2], up_grad.shape[3]
    rows = sources * most
    plane = n_x * n_y
    slots = n_lo * most
    low = lax.axis_index(HI) == 0
    rings = mirror_rings(sizes)
    ring_axes = (HI, CORE, LO)

    grad = jnp.transpose(up_grad[0, 0], (1, 0, 2)).reshape(rows, 2 * half)
    grad_own = jnp.where(low, grad[:, :half], grad[:, half:])
    grad_send = jnp.where(low, grad[:, half:], grad[:, :half])
    grad_mirror = lax.ppermute(grad_send, AXES, mirror_pairs(sizes))

    place = jnp.arange(rows, dtype=jnp.int32)
    at_x, at_y = place // (n_y * slots), (place // slots) % n_y
    at_lo, at_slot = (place // most) % n_lo, place % most
    taken = at_slot * sources + (at_x * n_lo + at_lo) * n_y + at_y
    order = (taken[:, None] == place[None, :]).astype(jnp.bfloat16)
    own_rows = dot(order, grad_own, ((1,), (0,))).astype(jnp.bfloat16)
    mirror_rows = dot(order, grad_mirror, ((1,), (0,))).astype(jnp.bfloat16)

    def exchange(value):
        value = value.reshape(plane, slots, width)
        return lax.all_to_all(value, (X, Y), 0, 0, tiled=True).reshape(rows, width)

    own_out = dot(own_rows, weight, ((1,), (1,))).astype(jnp.bfloat16)
    own_back = exchange(own_out)
    mirror_out = dot(mirror_rows, weight, ((1,), (1,))).astype(jnp.bfloat16)
    mirror_back = exchange(mirror_out)

    ids = lax.all_gather(expert_ids[0].T, ring_axes, axis=0, axis_index_groups=rings)
    gathered = lax.all_gather(token_rows, ring_axes, axis=0, axis_index_groups=rings, tiled=True)
    ids = ids.reshape(n_hi, n_lo, expert_ids.shape[2], count)
    member = jnp.arange(plane, dtype=jnp.int32)
    expert = ((member // n_y) * n_lo + lax.axis_index(LO)) * n_y + member % n_y
    named = jnp.any(ids[:, :, None] == expert[None, None, :, None, None], axis=3)
    earlier = jnp.arange(count)[:, None] < jnp.arange(count)[None, :]
    before = dot(named.astype(jnp.bfloat16), earlier.astype(jnp.bfloat16), ((3,), (0,)))
    source = jnp.arange(n_lo, dtype=jnp.int32)[None, :, None, None]
    key = jnp.where(named, source * most + before.astype(jnp.int32), -1)
    key = jnp.where(named & (before < most), key, -1)
    key = jnp.transpose(key, (0, 2, 1, 3)).reshape(n_hi, plane, n_lo * count)

    def selector(some):
        slot = jnp.arange(slots, dtype=jnp.int32)[None, :, None]
        return (some[:, None, :] == slot).astype(jnp.bfloat16).reshape(rows, n_lo * count)

    key_own = jnp.where(low, key[0], key[1])
    key_mirror = jnp.where(low, key[1], key[0])
    sums_own = dot(selector(key_own), own_back, ((0,), (0,))).astype(jnp.bfloat16)
    sums_mirror = dot(selector(key_mirror), mirror_back, ((0,), (0,))).astype(jnp.bfloat16)
    sums = jnp.concatenate(
        [jnp.where(low, sums_own, sums_mirror), jnp.where(low, sums_mirror, sums_own)]
    )
    token_grad = lax.psum_scatter(
        sums, ring_axes, scatter_dimension=0, axis_index_groups=rings, tiled=True
    )

    per_section = n_lo * count
    sent_first = dot(selector(key[0]), gathered[:per_section], ((1,), (0,))).astype(jnp.bfloat16)
    sent_second = dot(selector(key[1]), gathered[per_section:], ((1,), (0,))).astype(jnp.bfloat16)
    arrived_first = exchange(sent_first)
    arrived_second = exchange(sent_second)
    rows_first = jnp.where(low, own_rows, mirror_rows)
    rows_second = jnp.where(low, mirror_rows, own_rows)
    total = dot(arrived_first, rows_first, ((0,), (0,)))
    total = total + dot(arrived_second, rows_second, ((0,), (0,)))
    return (token_grad[None], total.astype(jnp.bfloat16)[None, None])


def solution(mesh):
    sizes = (2, 2, 4, 4, 4)
    fine = Mesh(mesh.devices.reshape(sizes), AXES)
    pipe, expert = (HI, CORE), (X, LO, Y)

    def device_body(*args):
        return on_device(sizes, *args)

    return jax.shard_map(
        device_body,
        mesh=fine,
        in_specs=(
            P(pipe, expert, None),
            P(pipe, expert, None),
            P(pipe, expert, None, None),
            P(pipe, expert, None, None, None),
        ),
        out_specs=(P(pipe, expert, None), P(pipe, expert, None, None)),
        check_vma=False,
    )
```

```python
import functools

import jax
import jax.numpy as jnp
from jax import lax
from jax.experimental import pallas as pl
from jax.experimental.pallas import tpu as pltpu
from jax.sharding import Mesh, PartitionSpec as P


HI, CORE, X, LO, Y = "hi", "core", "x", "lo", "y"
AXES = (HI, CORE, X, LO, Y)


def mirror_pairs(sizes):
    n_hi, n_core, n_x, n_lo, n_y = sizes
    block = n_x * n_lo * n_y
    pairs = []
    for section in range(n_hi * n_core):
        for place in range(block):
            pairs.append((section * block + place, (n_hi * n_core - 1 - section) * block + place))
    return pairs


def mirror_rings(sizes):
    n_hi, n_core, _, n_lo, _ = sizes
    return [
        [(hi * n_core + (core ^ hi)) * n_lo + lo for hi in range(n_hi) for lo in range(n_lo)]
        for core in range(n_core)
    ]


def shifted(value, axis, size, by):
    if by == 0:
        return value
    return lax.ppermute(value, axis, [(i, (i + by) % size) for i in range(size)])


def dot(a, b, dims):
    return lax.dot_general(a, b, (dims, ((), ())), preferred_element_type=jnp.float32)


def hidden_sum_kernel(*refs):
    grads, out = refs[0], refs[-1]
    total = None
    for i, piece in enumerate(refs[1:-1]):
        part = jnp.dot(grads[i], piece[...], preferred_element_type=jnp.float32)
        total = part if total is None else total + part
    out[...] = total.T.astype(out.dtype)


def hidden_sum(grads, pieces):
    count, half, depth = grads.shape
    width = pieces[0].shape[1]
    tile = 512 if width % 512 == 0 else width
    return pl.pallas_call(
        hidden_sum_kernel,
        out_shape=jax.ShapeDtypeStruct((width, half), jnp.bfloat16),
        grid=(width // tile,),
        in_specs=[pl.BlockSpec((count, half, depth), lambda i: (0, 0, 0))]
        + [pl.BlockSpec((depth, tile), lambda i: (0, i))] * count,
        out_specs=pl.BlockSpec((tile, half), lambda i: (i, 0)),
        name="hidden_sum",
    )(grads, *pieces)


def merge_kernel(*refs):
    out = refs[-1]
    size = refs[0].shape[0]
    for i, piece in enumerate(refs[:-1]):
        out[i * size : (i + 1) * size, :] = piece[...]


def merged(parts, step, size):
    width = parts[0].shape[1]
    tile = 896 if width % 896 == 0 else width
    return pl.pallas_call(
        merge_kernel,
        out_shape=jax.ShapeDtypeStruct((len(parts) * size, width), parts[0].dtype),
        grid=(width // tile,),
        in_specs=[pl.BlockSpec((size, tile), lambda i: (step, i))] * len(parts),
        out_specs=pl.BlockSpec((len(parts) * size, tile), lambda i: (0, i)),
        name="merged",
    )(*parts)


def key_kernel(sizes, most, top, place, ids, out, named_all):
    _, _, n_x, n_lo, n_y = sizes
    plane, count = n_x * n_y, ids.shape[2]
    my_x, my_lo, my_y = place[0], place[1], place[2]
    member = lax.broadcasted_iota(jnp.int32, (plane, count), 0)
    major, minor = member // n_y, member % n_y
    orders = (
        (0, (my_x + major) % n_x, (my_y + minor) % n_y),
        (1, (my_x + minor) % n_x, (my_y + major) % n_y),
        (0, major, minor),
        (1, major, minor),
    )
    for i, (hi, at_x, at_y) in enumerate(orders):
        expert = ((at_x * n_lo + my_lo) * n_y + at_y).astype(jnp.float32)
        for lo in range(n_lo):
            some = ids[hi * n_lo + lo].astype(jnp.float32)
            named = expert == some[0:1]
            for k in range(1, top):
                named = named | (expert == some[k : k + 1])
            row = (i * n_lo + lo) * plane
            named_all[row : row + plane, :] = jnp.where(named, 1.0, 0.0)
    token = lax.broadcasted_iota(jnp.int32, (count, count), 0)
    later = lax.broadcasted_iota(jnp.int32, (count, count), 1)
    earlier = jnp.where(token < later, 1.0, 0.0).astype(jnp.bfloat16)
    before = jnp.dot(
        named_all[...].astype(jnp.bfloat16), earlier, preferred_element_type=jnp.float32
    )
    for i in range(len(orders)):
        for lo in range(n_lo):
            row = (i * n_lo + lo) * plane
            slot = before[row : row + plane].astype(jnp.int32) + lo * most
            key = jnp.where(named_all[row : row + plane, :] > 0.5, slot, -1)
            out[i, :, lo * count : (lo + 1) * count] = key


def key_table(sizes, most, top, count, place, gathered):
    _, _, n_x, n_lo, n_y = sizes
    rings, per_source, _ = gathered.shape
    spare = per_source - count
    shape = (4, n_x * n_y, n_lo * count)
    return pl.pallas_call(
        functools.partial(key_kernel, sizes, most, top),
        out_shape=jax.ShapeDtypeStruct(shape, jnp.int32),
        grid=(1,),
        in_specs=[
            pl.BlockSpec(memory_space=pltpu.SMEM),
            pl.BlockSpec((rings, spare, count), lambda i: (0, count // spare, 0)),
        ],
        out_specs=pl.BlockSpec(shape, lambda i: (0, 0, 0)),
        scratch_shapes=[pltpu.VMEM((4 * n_lo * n_x * n_y, count), jnp.float32)],
        name="key_table",
    )(place, gathered)


def on_device(sizes, tokens, expert_ids, up_weight, up_grad):
    n_hi, _, n_x, n_lo, n_y = sizes
    token_rows = tokens[0]
    count, width = token_rows.shape
    weight = up_weight[0, 0]
    half = weight.shape[1]
    sources, most = up_grad.shape[2], up_grad.shape[3]
    top = expert_ids.shape[2]
    rows = sources * most
    plane = n_x * n_y
    slots = n_lo * most
    low = lax.axis_index(HI) == 0
    rings = mirror_rings(sizes)
    ring_axes = (HI, CORE, LO)
    bf16 = jnp.bfloat16
    spare = 8

    grad = jnp.transpose(up_grad[0, 0], (1, 0, 2)).reshape(rows, 2 * half)
    grad_own = jnp.where(low, grad[:, :half], grad[:, half:])
    grad_send = jnp.where(low, grad[:, half:], grad[:, :half])
    grad_mirror = lax.ppermute(grad_send, AXES, mirror_pairs(sizes))

    id_rows = jnp.pad(expert_ids[0].T.astype(bf16), ((0, spare - top), (0, width - count)))
    outgoing = jnp.concatenate([token_rows, id_rows])
    gathered = lax.all_gather(outgoing, ring_axes, axis=0, axis_index_groups=rings, tiled=True)

    def order(place, at_x, at_y):
        at_lo, at_slot = (place // most) % n_lo, place % most
        taken = at_slot * sources + (at_x * n_lo + at_lo) * n_y + at_y
        return (taken[:, None] == place[None, :]).astype(bf16)

    place = jnp.arange(rows, dtype=jnp.int32)
    by_place = order(place, place // (n_y * slots), (place // slots) % n_y)

    def row_grad(grads):
        sorted_rows = dot(by_place, grads, ((1,), (0,))).astype(bf16)
        return dot(sorted_rows, weight, ((1,), (1,))).astype(bf16)

    def exchange(value):
        value = value.reshape(plane, slots, width)
        return lax.all_to_all(value, (X, Y), 0, 0, tiled=True).reshape(rows, width)

    own_out = row_grad(grad_own)
    own_back = exchange(own_out)
    own_back, grad_mirror = lax.optimization_barrier((own_back, grad_mirror))
    mirror_out = row_grad(grad_mirror)
    mirror_back = exchange(mirror_out)
    my_x, my_lo, my_y = lax.axis_index(X), lax.axis_index(LO), lax.axis_index(Y)
    own_back, mirror_back, grad_own, grad_mirror, gathered, my_x, my_lo, my_y, nil = (
        lax.optimization_barrier(
            (own_back, mirror_back, grad_own, grad_mirror, gathered, my_x, my_lo, my_y, jnp.int32(0))
        )
    )

    per_source = count + spare
    keys = key_table(
        sizes,
        most,
        top,
        count,
        jnp.stack([my_x, my_lo, my_y]).astype(jnp.int32),
        gathered.reshape(n_hi * n_lo, per_source, width),
    )
    spaced = jnp.pad(
        keys[:2].reshape(2, plane, n_lo, count),
        ((0, 0), (0, 0), (0, 0), (0, spare)),
        constant_values=-1,
    ).reshape(2, plane, n_lo * per_source)

    def selector(some):
        slot = (jnp.arange(slots, dtype=jnp.int32) + nil)[None, :, None]
        return (some[:, None, :] == slot).astype(bf16).reshape(-1, some.shape[1])

    per_section = n_lo * per_source
    near_first, near_second = [None] * n_x, [None] * n_y
    for step in (1, 3, 2, 0):
        for key, which, near, axis, size in (
            (spaced[0], 0, near_first, X, n_x),
            (spaced[1], 1, near_second, Y, n_y),
        ):
            some = selector(key[step * (plane // size) : (step + 1) * (plane // size)])
            section = gathered[which * per_section : (which + 1) * per_section]
            sent = dot(some, section, ((1,), (0,))).astype(bf16)
            near[step] = shifted(sent, axis, size, step)

    key_own = jnp.where(low, keys[2], keys[3])
    key_mirror = jnp.where(low, keys[3], keys[2])
    sums_own = dot(selector(key_own), own_back, ((0,), (0,))).astype(bf16)
    sums_mirror = dot(selector(key_mirror), mirror_back, ((0,), (0,))).astype(bf16)
    sums = jnp.concatenate(
        [jnp.where(low, sums_own, sums_mirror), jnp.where(low, sums_mirror, sums_own)]
    )
    token_grad = lax.psum_scatter(
        sums, ring_axes, scatter_dimension=0, axis_index_groups=rings, tiled=True
    )

    grad_first = jnp.where(low, grad_own, grad_mirror)
    grad_second = jnp.where(low, grad_mirror, grad_own)
    late = place + nil
    outer, inner = late // (n_y * slots), (late // slots) % n_y
    order_first = order(late, (my_x - inner) % n_x, (my_y - outer) % n_y).reshape(n_y, -1, rows)
    order_second = order(late, (my_x - outer) % n_x, (my_y - inner) % n_y).reshape(n_x, -1, rows)
    turned_grad = jnp.concatenate(
        [
            jnp.einsum("rf,kcr->kfc", some, by, preferred_element_type=jnp.float32)
            for some, by in ((grad_first, order_first), (grad_second, order_second))
        ]
    ).astype(bf16)

    far_first, far_second = [None] * n_y, [None] * n_x
    for step in (1, 3, 2, 0):
        far_first[step] = shifted(merged(near_first, step, slots), Y, n_y, step)
        far_second[step] = shifted(merged(near_second, step, slots), X, n_x, step)
    weight_grad = hidden_sum(turned_grad, far_first + far_second)
    return (token_grad[None], weight_grad[None, None])


def solution(mesh):
    sizes = (2, 2, 4, 4, 4)
    fine = Mesh(mesh.devices.reshape(sizes), AXES)
    pipe, expert = (HI, CORE), (X, LO, Y)

    def device_body(*args):
        return on_device(sizes, *args)

    return jax.shard_map(
        device_body,
        mesh=fine,
        in_specs=(
            P(pipe, expert, None),
            P(pipe, expert, None),
            P(pipe, expert, None, None),
            P(pipe, expert, None, None, None),
        ),
        out_specs=(P(pipe, expert, None), P(pipe, expert, None, None)),
        check_vma=False,
    )
```

```python
import functools

import jax
import jax.numpy as jnp
from jax import lax
from jax.experimental import pallas as pl
from jax.experimental.pallas import tpu as pltpu
from jax.sharding import Mesh, PartitionSpec as P


HI, CORE, X, LO, Y = "hi", "core", "x", "lo", "y"
AXES = (HI, CORE, X, LO, Y)


def mirror_pairs(sizes):
    n_hi, n_core, n_x, n_lo, n_y = sizes
    block = n_x * n_lo * n_y
    pairs = []
    for section in range(n_hi * n_core):
        for place in range(block):
            pairs.append((section * block + place, (n_hi * n_core - 1 - section) * block + place))
    return pairs


def mirror_rings(sizes):
    n_hi, n_core, _, n_lo, _ = sizes
    return [
        [(hi * n_core + (core ^ hi)) * n_lo + lo for hi in range(n_hi) for lo in range(n_lo)]
        for core in range(n_core)
    ]


def shifted(value, axis, size, by):
    if by == 0:
        return value
    return lax.ppermute(value, axis, [(i, (i + by) % size) for i in range(size)])


def dot(a, b, dims):
    return lax.dot_general(a, b, (dims, ((), ())), preferred_element_type=jnp.float32)


def hidden_sum_kernel(tile, *refs):
    grads, pieces, out, block, arrived = refs[0], refs[1:-3], refs[-3], refs[-2], refs[-1]
    step, steps = pl.program_id(0), pl.num_programs(0)
    depth = pieces[0].shape[0]

    def copies(at, slot):
        columns = pl.ds(pl.multiple_of(at * tile, tile), tile)
        return [
            pltpu.make_async_copy(
                piece.at[:, columns],
                block.at[slot, i * depth : (i + 1) * depth],
                arrived.at[slot, i],
            )
            for i, piece in enumerate(pieces)
        ]

    @pl.when(step == 0)
    def _():
        for copy in copies(0, 0):
            copy.start()

    @pl.when(step + 1 < steps)
    def _():
        for copy in copies(step + 1, (step + 1) % 2):
            copy.start()

    for copy in copies(step, step % 2):
        copy.wait()
    total = jnp.dot(grads[...], block[step % 2], preferred_element_type=jnp.float32)
    out[...] = total.T.astype(out.dtype)


def hidden_sum(grads, pieces):
    half, rows = grads.shape
    _, width = pieces[0].shape
    tile = 512 if width % 512 == 0 else width
    return pl.pallas_call(
        functools.partial(hidden_sum_kernel, tile),
        out_shape=jax.ShapeDtypeStruct((width, half), jnp.bfloat16),
        grid=(width // tile,),
        in_specs=[pl.BlockSpec((half, rows), lambda i: (0, 0))]
        + [pl.BlockSpec(memory_space=pl.ANY)] * len(pieces),
        out_specs=pl.BlockSpec((tile, half), lambda i: (i, 0)),
        scratch_shapes=[
            pltpu.VMEM((2, rows, tile), jnp.bfloat16),
            pltpu.SemaphoreType.DMA((2, len(pieces))),
        ],
        name="hidden_sum",
    )(grads, *pieces)


def merge_kernel(size, *refs):
    count = (len(refs) - 1) // 2
    parts, outs, arrived = refs[:count], refs[count:-1], refs[-1]
    copies = []
    for step in range(len(outs)):
        for i, part in enumerate(parts):
            copies.append(
                pltpu.make_async_copy(
                    part.at[step * size : (step + 1) * size],
                    outs[step].at[i * size : (i + 1) * size],
                    arrived.at[step, i],
                )
            )
    for copy in copies:
        copy.start()
    for copy in copies:
        copy.wait()


def merged(parts, size):
    count = len(parts)
    return pl.pallas_call(
        functools.partial(merge_kernel, size),
        out_shape=[jax.ShapeDtypeStruct(parts[0].shape, parts[0].dtype)] * count,
        in_specs=[pl.BlockSpec(memory_space=pl.ANY)] * count,
        out_specs=[pl.BlockSpec(memory_space=pl.ANY)] * count,
        scratch_shapes=[pltpu.SemaphoreType.DMA((count, count))],
        name="merged",
    )(*parts)


def key_kernel(sizes, most, top, place, ids, out, named_all):
    _, _, n_x, n_lo, n_y = sizes
    plane, count = n_x * n_y, ids.shape[2]
    my_x, my_lo, my_y = place[0], place[1], place[2]
    member = lax.broadcasted_iota(jnp.int32, (plane, count), 0)
    major, minor = member // n_y, member % n_y
    orders = (
        (0, (my_x + major) % n_x, (my_y + minor) % n_y),
        (1, (my_x + minor) % n_x, (my_y + major) % n_y),
        (0, major, minor),
        (1, major, minor),
    )
    for i, (hi, at_x, at_y) in enumerate(orders):
        expert = ((at_x * n_lo + my_lo) * n_y + at_y).astype(jnp.float32)
        for lo in range(n_lo):
            some = ids[hi * n_lo + lo].astype(jnp.float32)
            named = expert == some[0:1]
            for k in range(1, top):
                named = named | (expert == some[k : k + 1])
            row = (i * n_lo + lo) * plane
            named_all[row : row + plane, :] = jnp.where(named, 1.0, 0.0)
    token = lax.broadcasted_iota(jnp.int32, (count, count), 0)
    later = lax.broadcasted_iota(jnp.int32, (count, count), 1)
    earlier = jnp.where(token < later, 1.0, 0.0).astype(jnp.bfloat16)
    before = jnp.dot(
        named_all[...].astype(jnp.bfloat16), earlier, preferred_element_type=jnp.float32
    )
    for i in range(len(orders)):
        for lo in range(n_lo):
            row = (i * n_lo + lo) * plane
            slot = before[row : row + plane].astype(jnp.int32) + lo * most
            key = jnp.where(named_all[row : row + plane, :] > 0.5, slot, -1)
            out[i, :, lo * count : (lo + 1) * count] = key


def key_table(sizes, most, top, count, place, gathered):
    _, _, n_x, n_lo, n_y = sizes
    rings, per_source, _ = gathered.shape
    spare = per_source - count
    shape = (4, n_x * n_y, n_lo * count)
    return pl.pallas_call(
        functools.partial(key_kernel, sizes, most, top),
        out_shape=jax.ShapeDtypeStruct(shape, jnp.int32),
        grid=(1,),
        in_specs=[
            pl.BlockSpec(memory_space=pltpu.SMEM),
            pl.BlockSpec((rings, spare, count), lambda i: (0, count // spare, 0)),
        ],
        out_specs=pl.BlockSpec(shape, lambda i: (0, 0, 0)),
        scratch_shapes=[pltpu.VMEM((4 * n_lo * n_x * n_y, count), jnp.float32)],
        name="key_table",
    )(place, gathered)


def on_device(sizes, tokens, expert_ids, up_weight, up_grad):
    n_hi, _, n_x, n_lo, n_y = sizes
    token_rows = tokens[0]
    count, width = token_rows.shape
    weight = up_weight[0, 0]
    half = weight.shape[1]
    sources, most = up_grad.shape[2], up_grad.shape[3]
    top = expert_ids.shape[2]
    rows = sources * most
    plane = n_x * n_y
    slots = n_lo * most
    low = lax.axis_index(HI) == 0
    rings = mirror_rings(sizes)
    ring_axes = (HI, CORE, LO)
    bf16 = jnp.bfloat16
    spare = 8

    grad = jnp.transpose(up_grad[0, 0], (1, 0, 2)).reshape(rows, 2 * half)
    place = jnp.arange(rows, dtype=jnp.int32)
    at_x, at_y = place // (n_y * slots), (place // slots) % n_y
    at_lo, at_slot = (place // most) % n_lo, place % most
    taken = at_slot * sources + (at_x * n_lo + at_lo) * n_y + at_y
    by_place = (taken[:, None] == place[None, :]).astype(bf16)
    grad = lax.optimization_barrier(dot(by_place, grad, ((1,), (0,))).astype(bf16))
    grad_own = jnp.where(low, grad[:, :half], grad[:, half:])
    grad_send = jnp.where(low, grad[:, half:], grad[:, :half])
    grad_mirror = lax.ppermute(grad_send, AXES, mirror_pairs(sizes))

    id_rows = jnp.pad(expert_ids[0].T.astype(bf16), ((0, spare - top), (0, width - count)))
    outgoing = jnp.concatenate([token_rows, id_rows])
    gathered = lax.all_gather(outgoing, ring_axes, axis=0, axis_index_groups=rings, tiled=True)

    def exchange(value):
        value = value.reshape(plane, slots, width)
        return lax.all_to_all(value, (X, Y), 0, 0, tiled=True).reshape(rows, width)

    my_x, my_lo, my_y = lax.axis_index(X), lax.axis_index(LO), lax.axis_index(Y)
    own_out = dot(grad_own, weight, ((1,), (1,))).astype(bf16)
    own_out, my_x, my_lo, my_y = lax.optimization_barrier((own_out, my_x, my_lo, my_y))
    own_back = exchange(own_out)
    own_back, grad_mirror = lax.optimization_barrier((own_back, grad_mirror))
    mirror_out = dot(grad_mirror, weight, ((1,), (1,))).astype(bf16)
    mirror_back = exchange(mirror_out)
    own_back, mirror_back, grad_own, grad_mirror, gathered, my_x, my_lo, my_y, nil = (
        lax.optimization_barrier(
            (own_back, mirror_back, grad_own, grad_mirror, gathered, my_x, my_lo, my_y, jnp.int32(0))
        )
    )

    per_source = count + spare
    keys = key_table(
        sizes,
        most,
        top,
        count,
        jnp.stack([my_x, my_lo, my_y]).astype(jnp.int32),
        gathered.reshape(n_hi * n_lo, per_source, width),
    )
    spaced = jnp.pad(
        keys[:2].reshape(2, plane, n_lo, count),
        ((0, 0), (0, 0), (0, 0), (0, spare)),
        constant_values=-1,
    ).reshape(2, plane, n_lo * per_source)

    def selector(some):
        slot = (jnp.arange(slots, dtype=jnp.int32) + nil)[None, :, None]
        return (some[:, None, :] == slot).astype(bf16).reshape(-1, some.shape[1])

    per_section = n_lo * per_source
    near_first, near_second = [None] * n_x, [None] * n_y
    for step in (1, 3, 2, 0):
        for key, which, near, axis, size in (
            (spaced[0], 0, near_first, X, n_x),
            (spaced[1], 1, near_second, Y, n_y),
        ):
            some = selector(key[step * (plane // size) : (step + 1) * (plane // size)])
            section = gathered[which * per_section : (which + 1) * per_section]
            sent = dot(some, section, ((1,), (0,))).astype(bf16)
            near[step] = shifted(sent, axis, size, step)

    key_own = jnp.where(low, keys[2], keys[3])
    key_mirror = jnp.where(low, keys[3], keys[2])
    sums_own = dot(selector(key_own), own_back, ((0,), (0,))).astype(bf16)
    sums_mirror = dot(selector(key_mirror), mirror_back, ((0,), (0,))).astype(bf16)
    sums = jnp.concatenate(
        [jnp.where(low, sums_own, sums_mirror), jnp.where(low, sums_mirror, sums_own)]
    )
    token_grad = lax.psum_scatter(
        sums, ring_axes, scatter_dimension=0, axis_index_groups=rings, tiled=True
    )

    far_first, far_second = [None] * n_y, [None] * n_x
    turned_first = merged(near_first, slots)
    turned_second = merged(near_second, slots)
    for step in (1, 3, 2, 0):
        far_first[step] = shifted(turned_first[step], Y, n_y, step)
        far_second[step] = shifted(turned_second[step], X, n_x, step)

    late = place + nil
    outer, inner, rest = late // (n_y * slots), (late // slots) % n_y, late % slots
    turned_grad = []
    for some, row_x, row_y in (
        (jnp.where(low, grad_own, grad_mirror), my_x - inner, my_y - outer),
        (jnp.where(low, grad_mirror, grad_own), my_x - outer, my_y - inner),
    ):
        row = ((row_x % n_x) * n_y + row_y % n_y) * slots + rest
        order = (place[:, None] == row[None, :]).astype(bf16)
        turned_grad.append(dot(some, order, ((0,), (0,))).astype(bf16))
    turned_grad = jnp.concatenate(turned_grad, axis=1)
    weight_grad = hidden_sum(turned_grad, far_first + far_second)
    return (token_grad[None], weight_grad[None, None])


def solution(mesh):
    sizes = (2, 2, 4, 4, 4)
    fine = Mesh(mesh.devices.reshape(sizes), AXES)
    pipe, expert = (HI, CORE), (X, LO, Y)

    def device_body(*args):
        return on_device(sizes, *args)

    return jax.shard_map(
        device_body,
        mesh=fine,
        in_specs=(
            P(pipe, expert, None),
            P(pipe, expert, None),
            P(pipe, expert, None, None),
            P(pipe, expert, None, None, None),
        ),
        out_specs=(P(pipe, expert, None), P(pipe, expert, None, None)),
        check_vma=False,
    )
```

```python
import functools

import jax
import jax.numpy as jnp
from jax import lax
from jax.experimental import pallas as pl
from jax.experimental.pallas import tpu as pltpu
from jax.sharding import Mesh, PartitionSpec as P


HI, CORE, X, LO, Y = "hi", "core", "x", "lo", "y"
AXES = (HI, CORE, X, LO, Y)


def mirror_pairs(sizes):
    n_hi, n_core, n_x, n_lo, n_y = sizes
    block = n_x * n_lo * n_y
    pairs = []
    for section in range(n_hi * n_core):
        for place in range(block):
            pairs.append((section * block + place, (n_hi * n_core - 1 - section) * block + place))
    return pairs


def mirror_rings(sizes):
    n_hi, n_core, _, n_lo, _ = sizes
    return [
        [(hi * n_core + (core ^ hi)) * n_lo + lo for hi in range(n_hi) for lo in range(n_lo)]
        for core in range(n_core)
    ]


def shifted(value, axis, size, by):
    if by == 0:
        return value
    return lax.ppermute(value, axis, [(i, (i + by) % size) for i in range(size)])


def dot(a, b, dims):
    return lax.dot_general(a, b, (dims, ((), ())), preferred_element_type=jnp.float32)


def hidden_sum_kernel(*refs):
    grads, pieces, out = refs[0], refs[1:9], refs[-1]
    total = None
    for i, piece in enumerate(pieces):
        part = lax.dot_general(
            piece[...], grads[i], (((0,), (0,)), ((), ())), preferred_element_type=jnp.float32
        )
        total = part if total is None else total + part
    out[...] = total.astype(out.dtype)


def hidden_sum(grads, pieces, part, parts, before):
    count, depth, half = grads.shape
    width = pieces[0].shape[1]
    tile = width // 2 if width % 256 == 0 else width
    steps = width // tile
    given = [] if before is None else [before]
    return pl.pallas_call(
        hidden_sum_kernel,
        out_shape=jax.ShapeDtypeStruct((parts * width, half), jnp.bfloat16),
        grid=(steps,),
        in_specs=[pl.BlockSpec((count, depth, half), lambda i: (0, 0, 0))]
        + [pl.BlockSpec((depth, tile), lambda i: (0, i))] * count
        + [pl.BlockSpec(memory_space=pl.ANY)] * len(given),
        out_specs=pl.BlockSpec((tile, half), lambda i: (part * steps + i, 0)),
        input_output_aliases={1 + count: 0} if given else {},
        name="hidden_sum",
    )(grads, *pieces, *given)


def merge_kernel(size, *refs):
    count = len(refs) // 2
    for step in range(count):
        for i in range(count):
            refs[count + step][i * size : (i + 1) * size, :] = refs[i][
                step * size : (step + 1) * size, :
            ]


def merged(parts, size):
    count = len(parts)
    rows, width = parts[0].shape
    tile = width // 2 if width % 256 == 0 else width
    block = pl.BlockSpec((rows, tile), lambda i: (0, i))
    return pl.pallas_call(
        functools.partial(merge_kernel, size),
        out_shape=[jax.ShapeDtypeStruct(parts[0].shape, parts[0].dtype)] * count,
        grid=(width // tile,),
        in_specs=[block] * count,
        out_specs=[block] * count,
        name="merged",
    )(*parts)


def pick_kernel(slots, keys, rows, *refs):
    outs, chosen = refs[:-1], refs[-1]
    total = keys.shape[2]

    @pl.when(pl.program_id(0) == 0)
    def _():
        slot = lax.broadcasted_iota(jnp.int32, (slots, total), 0)
        per_out = keys.shape[1] // len(outs)
        for k in range(len(outs)):
            some = [
                jnp.where(keys[0, k * per_out + m : k * per_out + m + 1, :] == slot, 1.0, 0.0)
                for m in range(per_out)
            ]
            chosen[k] = jnp.concatenate(some).astype(chosen.dtype)

    tokens = rows[...].reshape(total, rows.shape[2])
    for k, out in enumerate(outs):
        found = jnp.dot(chosen[k], tokens, preferred_element_type=jnp.float32)
        out[...] = found.astype(out.dtype)


def picked(keys, gathered, section, lo, count, slots, outs, part, parts):
    width = gathered.shape[2] // parts
    tile = width // 2 if width % 256 == 0 else width
    steps = width // tile
    total = lo * count
    per_out = keys.shape[1] // outs * slots
    return pl.pallas_call(
        functools.partial(pick_kernel, slots),
        out_shape=[jax.ShapeDtypeStruct((per_out, width), gathered.dtype)] * outs,
        grid=(steps,),
        in_specs=[
            pl.BlockSpec((1, keys.shape[1], total), lambda i: (section, 0, 0)),
            pl.BlockSpec((lo, count, tile), lambda i: (section, 0, part * steps + i)),
        ],
        out_specs=[pl.BlockSpec((per_out, tile), lambda i: (0, i))] * outs,
        scratch_shapes=[pltpu.VMEM((outs, per_out, total), gathered.dtype)],
        name="picked",
    )(keys, gathered)


def key_kernel(sizes, most, top, place, ids, out, named_all):
    _, _, n_x, n_lo, n_y = sizes
    plane, count = n_x * n_y, ids.shape[2]
    my_x, my_lo, my_y = place[0], place[1], place[2]
    member = lax.broadcasted_iota(jnp.int32, (plane, count), 0)
    major, minor = member // n_y, member % n_y
    orders = (
        (0, (my_x + major) % n_x, (my_y + minor) % n_y),
        (1, (my_x + minor) % n_x, (my_y + major) % n_y),
        (0, major, minor),
        (1, major, minor),
    )
    for i, (hi, at_x, at_y) in enumerate(orders):
        expert = ((at_x * n_lo + my_lo) * n_y + at_y).astype(jnp.float32)
        for lo in range(n_lo):
            some = ids[hi * n_lo + lo].astype(jnp.float32)
            named = expert == some[0:1]
            for k in range(1, top):
                named = named | (expert == some[k : k + 1])
            row = (i * n_lo + lo) * plane
            named_all[row : row + plane, :] = jnp.where(named, 1.0, 0.0)
    token = lax.broadcasted_iota(jnp.int32, (count, count), 0)
    later = lax.broadcasted_iota(jnp.int32, (count, count), 1)
    earlier = jnp.where(token < later, 1.0, 0.0).astype(jnp.bfloat16)
    before = jnp.dot(
        named_all[...].astype(jnp.bfloat16), earlier, preferred_element_type=jnp.float32
    )
    for i in range(len(orders)):
        for lo in range(n_lo):
            row = (i * n_lo + lo) * plane
            slot = before[row : row + plane].astype(jnp.int32) + lo * most
            key = jnp.where(named_all[row : row + plane, :] > 0.5, slot, -1)
            out[i, :, lo * count : (lo + 1) * count] = key


def key_table(sizes, most, top, count, place, gathered):
    _, _, n_x, n_lo, n_y = sizes
    rings, per_source, _ = gathered.shape
    spare = per_source - count
    shape = (4, n_x * n_y, n_lo * count)
    return pl.pallas_call(
        functools.partial(key_kernel, sizes, most, top),
        out_shape=jax.ShapeDtypeStruct(shape, jnp.int32),
        grid=(1,),
        in_specs=[
            pl.BlockSpec(memory_space=pltpu.SMEM),
            pl.BlockSpec((rings, spare, count), lambda i: (0, count // spare, 0)),
        ],
        out_specs=pl.BlockSpec(shape, lambda i: (0, 0, 0)),
        scratch_shapes=[pltpu.VMEM((4 * n_lo * n_x * n_y, count), jnp.float32)],
        name="key_table",
    )(place, gathered)


def on_device(sizes, tokens, expert_ids, up_weight, up_grad):
    n_hi, _, n_x, n_lo, n_y = sizes
    token_rows = tokens[0]
    count, width = token_rows.shape
    weight = up_weight[0, 0]
    half = weight.shape[1]
    sources, most = up_grad.shape[2], up_grad.shape[3]
    top = expert_ids.shape[2]
    rows = sources * most
    plane = n_x * n_y
    slots = n_lo * most
    low = lax.axis_index(HI) == 0
    rings = mirror_rings(sizes)
    ring_axes = (HI, CORE, LO)
    bf16 = jnp.bfloat16
    spare = 8

    grad = jnp.transpose(up_grad[0, 0], (1, 0, 2)).reshape(rows, 2 * half)
    place = jnp.arange(rows, dtype=jnp.int32)
    at_x, at_y = place // (n_y * slots), (place // slots) % n_y
    at_lo, at_slot = (place // most) % n_lo, place % most
    taken = at_slot * sources + (at_x * n_lo + at_lo) * n_y + at_y
    by_place = (taken[:, None] == place[None, :]).astype(bf16)
    grad = lax.optimization_barrier(dot(by_place, grad, ((1,), (0,))).astype(bf16))
    grad_own = jnp.where(low, grad[:, :half], grad[:, half:])
    grad_send = jnp.where(low, grad[:, half:], grad[:, :half])
    grad_mirror = lax.ppermute(grad_send, AXES, mirror_pairs(sizes))

    id_rows = jnp.pad(expert_ids[0].T.astype(bf16), ((0, spare - top), (0, width - count)))
    outgoing = jnp.concatenate([token_rows, id_rows])
    gathered = lax.all_gather(outgoing, ring_axes, axis=0, axis_index_groups=rings, tiled=True)

    def exchange(value):
        value = value.reshape(plane, slots, width)
        return lax.all_to_all(value, (X, Y), 0, 0, tiled=True).reshape(rows, width)

    my_x, my_lo, my_y = lax.axis_index(X), lax.axis_index(LO), lax.axis_index(Y)
    own_out = dot(grad_own, weight, ((1,), (1,))).astype(bf16)
    own_out, my_x, my_lo, my_y = lax.optimization_barrier((own_out, my_x, my_lo, my_y))
    own_back = exchange(own_out)
    own_back, grad_mirror = lax.optimization_barrier((own_back, grad_mirror))
    mirror_out = dot(grad_mirror, weight, ((1,), (1,))).astype(bf16)
    mirror_back = exchange(mirror_out)
    own_back, mirror_back, grad_own, grad_mirror, gathered, my_x, my_lo, my_y, nil = (
        lax.optimization_barrier(
            (own_back, mirror_back, grad_own, grad_mirror, gathered, my_x, my_lo, my_y, jnp.int32(0))
        )
    )

    gathered = gathered.reshape(n_hi * n_lo, count + spare, width)
    position = jnp.stack([my_x, my_lo, my_y]).astype(jnp.int32)
    keys = key_table(sizes, most, top, count, position, gathered)

    def selector(some):
        slot = (jnp.arange(slots, dtype=jnp.int32) + nil)[None, :, None]
        return (some[:, None, :] == slot).astype(bf16).reshape(-1, some.shape[1])

    parts = 2
    routes = ((X, n_x, Y, n_y), (Y, n_y, X, n_x))
    near = {}
    for part in range(parts):
        for section, (axis, size, _, _) in enumerate(routes):
            sent = picked(keys, gathered, section, n_lo, count, slots, size, part, parts)
            near[part, section] = [shifted(sent[i], axis, size, i) for i in range(size)]

    key_own = jnp.where(low, keys[2], keys[3])
    key_mirror = jnp.where(low, keys[3], keys[2])
    sums_own = dot(selector(key_own), own_back, ((0,), (0,))).astype(bf16)
    sums_mirror = dot(selector(key_mirror), mirror_back, ((0,), (0,))).astype(bf16)
    sums = jnp.concatenate(
        [jnp.where(low, sums_own, sums_mirror), jnp.where(low, sums_mirror, sums_own)]
    )
    token_grad = lax.psum_scatter(
        sums, ring_axes, scatter_dimension=0, axis_index_groups=rings, tiled=True
    )

    far = {}
    for part in range(parts):
        for section, (_, _, axis, size) in enumerate(routes):
            turned = merged(near[part, section], slots)
            far[part, section] = [shifted(turned[i], axis, size, i) for i in range(size)]

    late = place + nil
    outer, inner, rest = late // (n_y * slots), (late // slots) % n_y, late % slots
    turned_grad = []
    for some, row_x, row_y in (
        (jnp.where(low, grad_own, grad_mirror), my_x - inner, my_y - outer),
        (jnp.where(low, grad_mirror, grad_own), my_x - outer, my_y - inner),
    ):
        row = ((row_x % n_x) * n_y + row_y % n_y) * slots + rest
        order = (row[:, None] == place[None, :]).astype(bf16)
        turned_grad.append(dot(order, some, ((1,), (0,))).astype(bf16))
    turned_grad = jnp.concatenate(turned_grad).reshape(n_y + n_x, -1, half)
    weight_grad = None
    for part in range(parts):
        pieces = far[part, 0] + far[part, 1]
        weight_grad = hidden_sum(turned_grad, pieces, part, parts, weight_grad)
    return (token_grad[None], weight_grad[None, None])


def solution(mesh):
    sizes = (2, 2, 4, 4, 4)
    fine = Mesh(mesh.devices.reshape(sizes), AXES)
    pipe, expert = (HI, CORE), (X, LO, Y)

    def device_body(*args):
        return on_device(sizes, *args)

    return jax.shard_map(
        device_body,
        mesh=fine,
        in_specs=(
            P(pipe, expert, None),
            P(pipe, expert, None),
            P(pipe, expert, None, None),
            P(pipe, expert, None, None, None),
        ),
        out_specs=(P(pipe, expert, None), P(pipe, expert, None, None)),
        check_vma=False,
    )
```

```python
import functools

import jax
import jax.numpy as jnp
from jax import lax
from jax.experimental import pallas as pl
from jax.experimental.pallas import tpu as pltpu
from jax.sharding import Mesh, PartitionSpec as P


HI, CORE, X, LO, Y = "hi", "core", "x", "lo", "y"
AXES = (HI, CORE, X, LO, Y)


def mirror_pairs(sizes):
    count = sizes[0] * sizes[1]
    return [[section, count - 1 - section] for section in range(count // 2)]


def mirror_rings(sizes):
    n_hi, n_core, _, n_lo, _ = sizes
    return [
        [(hi * n_core + (core ^ hi)) * n_lo + lo for hi in range(n_hi) for lo in range(n_lo)]
        for core in range(n_core)
    ]


def shifted(value, axis, size, by):
    if by == 0:
        return value
    return lax.ppermute(value, axis, [(i, (i + by) % size) for i in range(size)])


def dot(a, b, dims):
    return lax.dot_general(a, b, (dims, ((), ())), preferred_element_type=jnp.float32)


def hidden_sum_kernel(*refs):
    grads, pieces, out = refs[0], refs[1:9], refs[-1]
    total = None
    for i, piece in enumerate(pieces):
        part = lax.dot_general(
            piece[...], grads[i], (((0,), (0,)), ((), ())), preferred_element_type=jnp.float32
        )
        total = part if total is None else total + part
    out[...] = total.astype(out.dtype)


def hidden_sum(grads, pieces, part, parts, before):
    count, depth, half = grads.shape
    width = pieces[0].shape[1]
    tile = width // 2 if width % 256 == 0 else width
    steps = width // tile
    given = [] if before is None else [before]
    return pl.pallas_call(
        hidden_sum_kernel,
        out_shape=jax.ShapeDtypeStruct((parts * width, half), jnp.bfloat16),
        grid=(steps,),
        in_specs=[pl.BlockSpec((count, depth, half), lambda i: (0, 0, 0))]
        + [pl.BlockSpec((depth, tile), lambda i: (0, i))] * count
        + [pl.BlockSpec(memory_space=pl.ANY)] * len(given),
        out_specs=pl.BlockSpec((tile, half), lambda i: (part * steps + i, 0)),
        input_output_aliases={1 + count: 0} if given else {},
        name="hidden_sum",
    )(grads, *pieces, *given)


def merge_kernel(size, *refs):
    count = len(refs) // 2
    for step in range(count):
        for i in range(count):
            refs[count + step][i * size : (i + 1) * size, :] = refs[i][
                step * size : (step + 1) * size, :
            ]


def merged(parts, size):
    count = len(parts)
    rows, width = parts[0].shape
    tile = width // 2 if width % 256 == 0 else width
    block = pl.BlockSpec((rows, tile), lambda i: (0, i))
    return pl.pallas_call(
        functools.partial(merge_kernel, size),
        out_shape=[jax.ShapeDtypeStruct(parts[0].shape, parts[0].dtype)] * count,
        grid=(width // tile,),
        in_specs=[block] * count,
        out_specs=[block] * count,
        name="merged",
    )(*parts)


def pick_kernel(slots, per_out, blocks, keys, rows, *refs):
    outs, chosen = refs[:-1], refs[-1]
    total = keys.shape[2]

    @pl.when(pl.program_id(0) == 0)
    def _():
        slot = lax.broadcasted_iota(jnp.int32, (slots, total), 0)
        for k, block in enumerate(blocks):
            first = block * per_out
            some = [
                jnp.where(keys[0, m : m + 1, :] == slot, 1.0, 0.0)
                for m in range(first, first + per_out)
            ]
            chosen[k] = jnp.concatenate(some).astype(chosen.dtype)

    tokens = rows[...].reshape(total, rows.shape[2])
    for k, out in enumerate(outs):
        found = jnp.dot(chosen[k], tokens, preferred_element_type=jnp.float32)
        out[...] = found.astype(out.dtype)


def picked(keys, gathered, section, lo, count, slots, size, blocks, part, parts):
    width = gathered.shape[2] // parts
    tile = width // 2 if width % 256 == 0 else width
    steps = width // tile
    total = lo * count
    per_out = keys.shape[1] // size
    shape = (per_out * slots, width)
    return pl.pallas_call(
        functools.partial(pick_kernel, slots, per_out, blocks),
        out_shape=[jax.ShapeDtypeStruct(shape, gathered.dtype)] * len(blocks),
        grid=(steps,),
        in_specs=[
            pl.BlockSpec((1, keys.shape[1], total), lambda i: (section, 0, 0)),
            pl.BlockSpec((lo, count, tile), lambda i: (section, 0, part * steps + i)),
        ],
        out_specs=[pl.BlockSpec((shape[0], tile), lambda i: (0, i))] * len(blocks),
        scratch_shapes=[pltpu.VMEM((len(blocks), shape[0], total), gathered.dtype)],
        name="picked",
    )(keys, gathered)


def key_kernel(sizes, most, top, place, ids, out, named_all):
    _, _, n_x, n_lo, n_y = sizes
    plane, count = n_x * n_y, ids.shape[2]
    my_x, my_lo, my_y = place[0], place[1], place[2]
    member = lax.broadcasted_iota(jnp.int32, (plane, count), 0)
    major, minor = member // n_y, member % n_y
    orders = (
        (0, (my_x + major) % n_x, (my_y + minor) % n_y),
        (1, (my_x + minor) % n_x, (my_y + major) % n_y),
        (0, major, minor),
        (1, major, minor),
    )
    for i, (hi, at_x, at_y) in enumerate(orders):
        expert = ((at_x * n_lo + my_lo) * n_y + at_y).astype(jnp.float32)
        for lo in range(n_lo):
            some = ids[hi * n_lo + lo].astype(jnp.float32)
            named = expert == some[0:1]
            for k in range(1, top):
                named = named | (expert == some[k : k + 1])
            row = (i * n_lo + lo) * plane
            named_all[row : row + plane, :] = jnp.where(named, 1.0, 0.0)
    token = lax.broadcasted_iota(jnp.int32, (count, count), 0)
    later = lax.broadcasted_iota(jnp.int32, (count, count), 1)
    earlier = jnp.where(token < later, 1.0, 0.0).astype(jnp.bfloat16)
    before = jnp.dot(
        named_all[...].astype(jnp.bfloat16), earlier, preferred_element_type=jnp.float32
    )
    for i in range(len(orders)):
        for lo in range(n_lo):
            row = (i * n_lo + lo) * plane
            slot = before[row : row + plane].astype(jnp.int32) + lo * most
            key = jnp.where(named_all[row : row + plane, :] > 0.5, slot, -1)
            out[i, :, lo * count : (lo + 1) * count] = key


def key_table(sizes, most, top, count, place, gathered):
    _, _, n_x, n_lo, n_y = sizes
    rings, per_source, _ = gathered.shape
    spare = per_source - count
    shape = (4, n_x * n_y, n_lo * count)
    return pl.pallas_call(
        functools.partial(key_kernel, sizes, most, top),
        out_shape=jax.ShapeDtypeStruct(shape, jnp.int32),
        grid=(1,),
        in_specs=[
            pl.BlockSpec(memory_space=pltpu.SMEM),
            pl.BlockSpec((rings, spare, count), lambda i: (0, count // spare, 0)),
        ],
        out_specs=pl.BlockSpec(shape, lambda i: (0, 0, 0)),
        scratch_shapes=[pltpu.VMEM((4 * n_lo * n_x * n_y, count), jnp.float32)],
        name="key_table",
    )(place, gathered)


def on_device(sizes, tokens, expert_ids, up_weight, up_grad):
    n_hi, _, n_x, n_lo, n_y = sizes
    token_rows = tokens[0]
    count, width = token_rows.shape
    weight = up_weight[0, 0]
    half = weight.shape[1]
    sources, most = up_grad.shape[2], up_grad.shape[3]
    top = expert_ids.shape[2]
    rows = sources * most
    plane = n_x * n_y
    slots = n_lo * most
    low = lax.axis_index(HI) == 0
    rings = mirror_rings(sizes)
    ring_axes = (HI, CORE, LO)
    bf16 = jnp.bfloat16
    spare = 8

    grad = jnp.transpose(up_grad[0, 0], (1, 0, 2)).reshape(rows, 2 * half)
    place = jnp.arange(rows, dtype=jnp.int32)
    at_x, at_y = place // (n_y * slots), (place // slots) % n_y
    at_lo, at_slot = (place // most) % n_lo, place % most
    taken = at_slot * sources + (at_x * n_lo + at_lo) * n_y + at_y
    by_place = (taken[:, None] == place[None, :]).astype(bf16)
    grad = lax.optimization_barrier(dot(by_place, grad, ((1,), (0,))).astype(bf16))
    grad_own = jnp.where(low, grad[:, :half], grad[:, half:])
    grad_send = jnp.where(low, grad[:, half:], grad[:, :half])
    pair = (HI, CORE)
    swapped = lax.all_gather(grad_send, pair, axis=0, axis_index_groups=mirror_pairs(sizes))

    id_rows = jnp.pad(expert_ids[0].T.astype(bf16), ((0, spare - top), (0, width - count)))
    outgoing = jnp.concatenate([token_rows, id_rows])
    gathered = lax.all_gather(outgoing, ring_axes, axis=0, axis_index_groups=rings, tiled=True)

    def exchange(value):
        value = value.reshape(plane, slots, width)
        return lax.all_to_all(value, (X, Y), 0, 0, tiled=True).reshape(rows, width)

    my_x, my_lo, my_y = lax.axis_index(X), lax.axis_index(LO), lax.axis_index(Y)
    own_out = dot(grad_own, weight, ((1,), (1,))).astype(bf16)
    own_out, my_x, my_lo, my_y = lax.optimization_barrier((own_out, my_x, my_lo, my_y))
    own_back = exchange(own_out)
    own_back, swapped = lax.optimization_barrier((own_back, swapped))
    grad_mirror = jnp.where(low, swapped[1], swapped[0])
    mirror_out = dot(grad_mirror, weight, ((1,), (1,))).astype(bf16)
    mirror_back = exchange(mirror_out)
    own_back, mirror_back, grad_own, grad_mirror, gathered, my_x, my_lo, my_y, nil = (
        lax.optimization_barrier(
            (own_back, mirror_back, grad_own, grad_mirror, gathered, my_x, my_lo, my_y, jnp.int32(0))
        )
    )

    gathered = gathered.reshape(n_hi * n_lo, count + spare, width)
    position = jnp.stack([my_x, my_lo, my_y]).astype(jnp.int32)
    keys = key_table(sizes, most, top, count, position, gathered)

    def selector(some):
        slot = (jnp.arange(slots, dtype=jnp.int32) + nil)[None, :, None]
        return (some[:, None, :] == slot).astype(bf16).reshape(-1, some.shape[1])

    parts = 2
    routes = ((X, n_x, Y, n_y), (Y, n_y, X, n_x))
    near = {(part, section): [None] * n_x for part in range(parts) for section in range(n_hi)}
    turn = 0
    for part, blocks in ((0, (1,)), (0, (n_x - 1,)), (0, (2, 0)), (1, (1, n_x - 1, 2, 0))):
        for section, (axis, size, _, _) in enumerate(routes):
            sent = picked(keys, gathered, section, n_lo, count, slots, size, blocks, part, parts)
            for block, value in zip(blocks, sent):
                near[part, section][block] = shifted(value, axis, size, block)
            turn += 1

    key_own = jnp.where(low, keys[2], keys[3])
    key_mirror = jnp.where(low, keys[3], keys[2])
    sums_own = dot(selector(key_own), own_back, ((0,), (0,))).astype(bf16)
    sums_mirror = dot(selector(key_mirror), mirror_back, ((0,), (0,))).astype(bf16)
    sums = jnp.concatenate(
        [jnp.where(low, sums_own, sums_mirror), jnp.where(low, sums_mirror, sums_own)]
    )
    token_grad = lax.psum_scatter(
        sums, ring_axes, scatter_dimension=0, axis_index_groups=rings, tiled=True
    )

    far = {}
    for part in range(parts):
        for section, (_, _, axis, size) in enumerate(routes):
            turn = str(2 * part + section)
            turned = merged(near[part, section], slots)
            far[part, section] = [shifted(turned[i], axis, size, i) for i in range(size)]

    late = place + nil
    outer, inner, rest = late // (n_y * slots), (late // slots) % n_y, late % slots
    turned_grad = []
    for some, row_x, row_y in (
        (jnp.where(low, grad_own, grad_mirror), my_x - inner, my_y - outer),
        (jnp.where(low, grad_mirror, grad_own), my_x - outer, my_y - inner),
    ):
        row = ((row_x % n_x) * n_y + row_y % n_y) * slots + rest
        order = (row[:, None] == place[None, :]).astype(bf16)
        turned_grad.append(dot(order, some, ((1,), (0,))).astype(bf16))
    turned_grad = jnp.concatenate(turned_grad).reshape(n_y + n_x, -1, half)
    weight_grad = None
    for part in range(parts):
        pieces = far[part, 0] + far[part, 1]
        weight_grad = hidden_sum(turned_grad, pieces, part, parts, weight_grad)
    return (token_grad[None], weight_grad[None, None])


def solution(mesh):
    sizes = (2, 2, 4, 4, 4)
    fine = Mesh(mesh.devices.reshape(sizes), AXES)
    pipe, expert = (HI, CORE), (X, LO, Y)

    def device_body(*args):
        return on_device(sizes, *args)

    return jax.shard_map(
        device_body,
        mesh=fine,
        in_specs=(
            P(pipe, expert, None),
            P(pipe, expert, None),
            P(pipe, expert, None, None),
            P(pipe, expert, None, None, None),
        ),
        out_specs=(P(pipe, expert, None), P(pipe, expert, None, None)),
        check_vma=False,
    )
```

```python
import functools

import jax
import jax.numpy as jnp
from jax import lax
from jax.experimental import pallas as pl
from jax.experimental.pallas import tpu as pltpu
from jax.sharding import Mesh, PartitionSpec as P


HI, CORE, X, LO, Y = "hi", "core", "x", "lo", "y"
AXES = (HI, CORE, X, LO, Y)


def mirror_pairs(sizes):
    count = sizes[0] * sizes[1]
    return [[section, count - 1 - section] for section in range(count // 2)]


def mirror_rings(sizes):
    n_hi, n_core, _, n_lo, _ = sizes
    return [
        [(hi * n_core + (core ^ hi)) * n_lo + lo for hi in range(n_hi) for lo in range(n_lo)]
        for core in range(n_core)
    ]


def shifted(value, axis, size, by):
    if by == 0:
        return value
    return lax.ppermute(value, axis, [(i, (i + by) % size) for i in range(size)])


def dot(a, b, dims):
    return lax.dot_general(a, b, (dims, ((), ())), preferred_element_type=jnp.float32)


def hidden_sum_kernel(*refs):
    grads, pieces, out = refs[0], refs[1:9], refs[-1]
    total = None
    for i, piece in enumerate(pieces):
        part = lax.dot_general(
            piece[...], grads[i], (((0,), (0,)), ((), ())), preferred_element_type=jnp.float32
        )
        total = part if total is None else total + part
    out[...] = total.astype(out.dtype)


def hidden_sum(grads, pieces, part, parts, before):
    count, depth, half = grads.shape
    width = pieces[0].shape[1]
    tile = width // 2 if width % 256 == 0 else width
    steps = width // tile
    given = [] if before is None else [before]
    return pl.pallas_call(
        hidden_sum_kernel,
        out_shape=jax.ShapeDtypeStruct((parts * width, half), jnp.bfloat16),
        grid=(steps,),
        in_specs=[pl.BlockSpec((count, depth, half), lambda i: (0, 0, 0))]
        + [pl.BlockSpec((depth, tile), lambda i: (0, i))] * count
        + [pl.BlockSpec(memory_space=pl.ANY)] * len(given),
        out_specs=pl.BlockSpec((tile, half), lambda i: (part * steps + i, 0)),
        input_output_aliases={1 + count: 0} if given else {},
        name="hidden_sum",
    )(grads, *pieces, *given)


def merge_kernel(size, *refs):
    count = len(refs) // 2
    for step in range(count):
        for i in range(count):
            refs[count + step][i * size : (i + 1) * size, :] = refs[i][
                step * size : (step + 1) * size, :
            ]


def merged(parts, size):
    count = len(parts)
    rows, width = parts[0].shape
    tile = width // 2 if width % 256 == 0 else width
    block = pl.BlockSpec((rows, tile), lambda i: (0, i))
    return pl.pallas_call(
        functools.partial(merge_kernel, size),
        out_shape=[jax.ShapeDtypeStruct(parts[0].shape, parts[0].dtype)] * count,
        grid=(width // tile,),
        in_specs=[block] * count,
        out_specs=[block] * count,
        name="merged",
    )(*parts)


def pick_kernel(slots, per_out, blocks, keys, rows, *refs):
    outs, chosen = refs[:-1], refs[-1]
    total = keys.shape[2]

    @pl.when(pl.program_id(0) == 0)
    def _():
        slot = lax.broadcasted_iota(jnp.int32, (slots, total), 0)
        for k, block in enumerate(blocks):
            first = block * per_out
            some = [
                jnp.where(keys[0, m : m + 1, :] == slot, 1.0, 0.0)
                for m in range(first, first + per_out)
            ]
            chosen[k] = jnp.concatenate(some).astype(chosen.dtype)

    tokens = rows[...].reshape(total, rows.shape[2])
    for k, out in enumerate(outs):
        found = jnp.dot(chosen[k], tokens, preferred_element_type=jnp.float32)
        out[...] = found.astype(out.dtype)


def picked(keys, gathered, section, lo, count, slots, size, blocks, part, parts):
    width = gathered.shape[2] // parts
    tile = width // 2 if width % 256 == 0 else width
    steps = width // tile
    total = lo * count
    per_out = keys.shape[1] // size
    shape = (per_out * slots, width)
    return pl.pallas_call(
        functools.partial(pick_kernel, slots, per_out, blocks),
        out_shape=[jax.ShapeDtypeStruct(shape, gathered.dtype)] * len(blocks),
        grid=(steps,),
        in_specs=[
            pl.BlockSpec((1, keys.shape[1], total), lambda i: (section, 0, 0)),
            pl.BlockSpec((lo, count, tile), lambda i: (section, 0, part * steps + i)),
        ],
        out_specs=[pl.BlockSpec((shape[0], tile), lambda i: (0, i))] * len(blocks),
        scratch_shapes=[pltpu.VMEM((len(blocks), shape[0], total), gathered.dtype)],
        name="picked",
    )(keys, gathered)


def sum_kernel(slots, at, keys, rows, *refs):
    out, chosen = refs[-2], refs[-1]
    total = keys.shape[2]

    @pl.when(pl.program_id(0) == 0)
    def _():
        slot = lax.broadcasted_iota(jnp.int32, (slots, total), 0)
        some = [
            jnp.where(keys[0, m : m + 1, :] == slot, 1.0, 0.0) for m in range(keys.shape[1])
        ]
        chosen[...] = jnp.concatenate(some).T.astype(chosen.dtype)

    found = jnp.dot(chosen[...], rows[...], preferred_element_type=jnp.float32)
    out[...] = found.astype(out.dtype)


def token_sums(section, keys, rows, slots, before):
    count, width = rows.shape
    total = keys.shape[2]
    tile = width // 4 if width % 512 == 0 else width
    given = [] if before is None else [before]
    return pl.pallas_call(
        functools.partial(sum_kernel, slots),
        out_shape=jax.ShapeDtypeStruct((2 * total, width), rows.dtype),
        grid_spec=pltpu.PrefetchScalarGridSpec(
            num_scalar_prefetch=1,
            grid=(width // tile,),
            in_specs=[
                pl.BlockSpec((1, keys.shape[1], total), lambda i, at: (2 + at[0], 0, 0)),
                pl.BlockSpec((count, tile), lambda i, at: (0, i)),
            ]
            + [pl.BlockSpec(memory_space=pl.ANY)] * len(given),
            out_specs=pl.BlockSpec((total, tile), lambda i, at: (at[0], i)),
            scratch_shapes=[pltpu.VMEM((total, count), rows.dtype)],
        ),
        input_output_aliases={3: 0} if given else {},
        name="token_sums",
    )(section, keys, rows, *given)


def key_kernel(sizes, most, top, place, ids, out, named_all):
    _, _, n_x, n_lo, n_y = sizes
    plane, count = n_x * n_y, ids.shape[2]
    my_x, my_lo, my_y = place[0], place[1], place[2]
    member = lax.broadcasted_iota(jnp.int32, (plane, count), 0)
    major, minor = member // n_y, member % n_y
    orders = (
        (0, (my_x + major) % n_x, (my_y + minor) % n_y),
        (1, (my_x + minor) % n_x, (my_y + major) % n_y),
        (0, major, minor),
        (1, major, minor),
    )
    for i, (hi, at_x, at_y) in enumerate(orders):
        expert = ((at_x * n_lo + my_lo) * n_y + at_y).astype(jnp.float32)
        for lo in range(n_lo):
            some = ids[hi * n_lo + lo].astype(jnp.float32)
            named = expert == some[0:1]
            for k in range(1, top):
                named = named | (expert == some[k : k + 1])
            row = (i * n_lo + lo) * plane
            named_all[row : row + plane, :] = jnp.where(named, 1.0, 0.0)
    token = lax.broadcasted_iota(jnp.int32, (count, count), 0)
    later = lax.broadcasted_iota(jnp.int32, (count, count), 1)
    earlier = jnp.where(token < later, 1.0, 0.0).astype(jnp.bfloat16)
    before = jnp.dot(
        named_all[...].astype(jnp.bfloat16), earlier, preferred_element_type=jnp.float32
    )
    for i in range(len(orders)):
        for lo in range(n_lo):
            row = (i * n_lo + lo) * plane
            slot = before[row : row + plane].astype(jnp.int32) + lo * most
            key = jnp.where(named_all[row : row + plane, :] > 0.5, slot, -1)
            out[i, :, lo * count : (lo + 1) * count] = key


def key_table(sizes, most, top, count, place, gathered):
    _, _, n_x, n_lo, n_y = sizes
    rings, per_source, _ = gathered.shape
    spare = per_source - count
    shape = (4, n_x * n_y, n_lo * count)
    return pl.pallas_call(
        functools.partial(key_kernel, sizes, most, top),
        out_shape=jax.ShapeDtypeStruct(shape, jnp.int32),
        grid=(1,),
        in_specs=[
            pl.BlockSpec(memory_space=pltpu.SMEM),
            pl.BlockSpec((rings, spare, count), lambda i: (0, count // spare, 0)),
        ],
        out_specs=pl.BlockSpec(shape, lambda i: (0, 0, 0)),
        scratch_shapes=[pltpu.VMEM((4 * n_lo * n_x * n_y, count), jnp.float32)],
        name="key_table",
    )(place, gathered)


def on_device(sizes, tokens, expert_ids, up_weight, up_grad):
    n_hi, _, n_x, n_lo, n_y = sizes
    token_rows = tokens[0]
    count, width = token_rows.shape
    weight = up_weight[0, 0]
    half = weight.shape[1]
    sources, most = up_grad.shape[2], up_grad.shape[3]
    top = expert_ids.shape[2]
    rows = sources * most
    plane = n_x * n_y
    slots = n_lo * most
    low = lax.axis_index(HI) == 0
    rings = mirror_rings(sizes)
    ring_axes = (HI, CORE, LO)
    bf16 = jnp.bfloat16
    spare = 8

    grad = jnp.transpose(up_grad[0, 0], (1, 0, 2)).reshape(rows, 2 * half)
    place = jnp.arange(rows, dtype=jnp.int32)
    at_x, at_y = place // (n_y * slots), (place // slots) % n_y
    at_lo, at_slot = (place // most) % n_lo, place % most
    taken = at_slot * sources + (at_x * n_lo + at_lo) * n_y + at_y
    by_place = (taken[:, None] == place[None, :]).astype(bf16)
    grad = lax.optimization_barrier(dot(by_place, grad, ((1,), (0,))).astype(bf16))
    grad_own = jnp.where(low, grad[:, :half], grad[:, half:])
    grad_send = jnp.where(low, grad[:, half:], grad[:, :half])
    pair = (HI, CORE)
    swapped = lax.all_gather(grad_send, pair, axis=0, axis_index_groups=mirror_pairs(sizes))

    id_rows = jnp.pad(expert_ids[0].T.astype(bf16), ((0, spare - top), (0, width - count)))
    outgoing = jnp.concatenate([token_rows, id_rows])
    gathered = lax.all_gather(outgoing, ring_axes, axis=0, axis_index_groups=rings, tiled=True)

    def exchange(value):
        value = value.reshape(plane, slots, width)
        return lax.all_to_all(value, (X, Y), 0, 0, tiled=True).reshape(rows, width)

    my_hi, my_x = lax.axis_index(HI), lax.axis_index(X)
    my_lo, my_y = lax.axis_index(LO), lax.axis_index(Y)
    own_out = dot(grad_own, weight, ((1,), (1,))).astype(bf16)
    own_out, my_hi, my_x, my_lo, my_y = lax.optimization_barrier(
        (own_out, my_hi, my_x, my_lo, my_y)
    )
    own_back = exchange(own_out)
    own_back, swapped = lax.optimization_barrier((own_back, swapped))
    grad_mirror = jnp.where(low, swapped[1], swapped[0])
    mirror_out = dot(grad_mirror, weight, ((1,), (1,))).astype(bf16)
    mirror_back = exchange(mirror_out)
    own_back, mirror_back, grad_own, grad_mirror, gathered = lax.optimization_barrier(
        (own_back, mirror_back, grad_own, grad_mirror, gathered)
    )
    _, my_hi, my_x, my_lo, my_y, nil = lax.optimization_barrier(
        (mirror_back, my_hi, my_x, my_lo, my_y, jnp.int32(0))
    )

    gathered = gathered.reshape(n_hi * n_lo, count + spare, width)
    position = jnp.stack([my_x, my_lo, my_y]).astype(jnp.int32)
    keys = key_table(sizes, most, top, count, position, gathered)

    parts = 2
    routes = ((X, n_x, Y, n_y), (Y, n_y, X, n_x))
    near = {(part, section): [None] * n_x for part in range(parts) for section in range(n_hi)}
    turn = 0
    for part, blocks in ((0, (1, n_x - 1, 2, 0)), (1, (1, n_x - 1, 2, 0))):
        for section, (axis, size, _, _) in enumerate(routes):
            sent = picked(keys, gathered, section, n_lo, count, slots, size, blocks, part, parts)
            for block, value in zip(blocks, sent):
                near[part, section][block] = shifted(value, axis, size, block)
            turn += 1

    section = jnp.reshape(my_hi, (1,)).astype(jnp.int32)
    sums = token_sums(section, keys, own_back, slots, None)
    sums = token_sums(1 - section, keys, mirror_back, slots, sums)
    token_grad = lax.psum_scatter(
        sums, ring_axes, scatter_dimension=0, axis_index_groups=rings, tiled=True
    )

    far = {}
    for part in range(parts):
        for section, (_, _, axis, size) in enumerate(routes):
            turn = str(2 * part + section)
            turned = merged(near[part, section], slots)
            far[part, section] = [shifted(turned[i], axis, size, i) for i in range(size)]

    late = place + nil
    outer, inner, rest = late // (n_y * slots), (late // slots) % n_y, late % slots
    turned_grad = []
    for some, row_x, row_y in (
        (jnp.where(low, grad_own, grad_mirror), my_x - inner, my_y - outer),
        (jnp.where(low, grad_mirror, grad_own), my_x - outer, my_y - inner),
    ):
        row = ((row_x % n_x) * n_y + row_y % n_y) * slots + rest
        order = (row[:, None] == place[None, :]).astype(bf16)
        turned_grad.append(dot(order, some, ((1,), (0,))).astype(bf16))
    turned_grad = jnp.concatenate(turned_grad).reshape(n_y + n_x, -1, half)
    weight_grad = None
    for part in range(parts):
        pieces = far[part, 0] + far[part, 1]
        weight_grad = hidden_sum(turned_grad, pieces, part, parts, weight_grad)
    return (token_grad[None], weight_grad[None, None])


def solution(mesh):
    sizes = (2, 2, 4, 4, 4)
    fine = Mesh(mesh.devices.reshape(sizes), AXES)
    pipe, expert = (HI, CORE), (X, LO, Y)

    def device_body(*args):
        return on_device(sizes, *args)

    return jax.shard_map(
        device_body,
        mesh=fine,
        in_specs=(
            P(pipe, expert, None),
            P(pipe, expert, None),
            P(pipe, expert, None, None),
            P(pipe, expert, None, None, None),
        ),
        out_specs=(P(pipe, expert, None), P(pipe, expert, None, None)),
        check_vma=False,
    )
```

```python
import functools

import jax
import jax.numpy as jnp
from jax import lax
from jax.experimental import pallas as pl
from jax.experimental.pallas import tpu as pltpu
from jax.sharding import Mesh, PartitionSpec as P


HI, CORE, X, LO, Y = "hi", "core", "x", "lo", "y"
AXES = (HI, CORE, X, LO, Y)


def mirror_pairs(sizes):
    count = sizes[0] * sizes[1]
    return [[section, count - 1 - section] for section in range(count // 2)]


def mirror_rings(sizes):
    n_hi, n_core, _, n_lo, _ = sizes
    return [
        [(hi * n_core + (core ^ hi)) * n_lo + lo for hi in range(n_hi) for lo in range(n_lo)]
        for core in range(n_core)
    ]


def shifted(value, axis, size, by):
    if by == 0:
        return value
    return lax.ppermute(value, axis, [(i, (i + by) % size) for i in range(size)])


def dot(a, b, dims):
    return lax.dot_general(a, b, (dims, ((), ())), preferred_element_type=jnp.float32)


def hidden_sum_kernel(*refs):
    grads, pieces, out = refs[0], refs[1:9], refs[-1]
    total = None
    for i, piece in enumerate(pieces):
        part = lax.dot_general(
            piece[...], grads[i], (((0,), (0,)), ((), ())), preferred_element_type=jnp.float32
        )
        total = part if total is None else total + part
    out[...] = total.astype(out.dtype)


def hidden_sum(grads, pieces, part, parts, before):
    count, depth, half = grads.shape
    width = pieces[0].shape[1]
    tile = width // 2 if width % 256 == 0 else width
    steps = width // tile
    given = [] if before is None else [before]
    return pl.pallas_call(
        hidden_sum_kernel,
        out_shape=jax.ShapeDtypeStruct((parts * width, half), jnp.bfloat16),
        grid=(steps,),
        in_specs=[pl.BlockSpec((count, depth, half), lambda i: (0, 0, 0))]
        + [pl.BlockSpec((depth, tile), lambda i: (0, i))] * count
        + [pl.BlockSpec(memory_space=pl.ANY)] * len(given),
        out_specs=pl.BlockSpec((tile, half), lambda i: (part * steps + i, 0)),
        input_output_aliases={1 + count: 0} if given else {},
        name="hidden_sum",
    )(grads, *pieces, *given)


def merge_kernel(size, *refs):
    count = len(refs) // 2
    for step in range(count):
        for i in range(count):
            refs[count + step][i * size : (i + 1) * size, :] = refs[i][
                step * size : (step + 1) * size, :
            ]


def merged(parts, size):
    count = len(parts)
    rows, width = parts[0].shape
    tile = width // 2 if width % 256 == 0 else width
    block = pl.BlockSpec((rows, tile), lambda i: (0, i))
    return pl.pallas_call(
        functools.partial(merge_kernel, size),
        out_shape=[jax.ShapeDtypeStruct(parts[0].shape, parts[0].dtype)] * count,
        grid=(width // tile,),
        in_specs=[block] * count,
        out_specs=[block] * count,
        name="merged",
    )(*parts)


def pick_kernel(slots, per_out, blocks, keys, rows, *refs):
    outs, chosen = refs[:-1], refs[-1]
    total = keys.shape[2]

    @pl.when(pl.program_id(0) == 0)
    def _():
        slot = lax.broadcasted_iota(jnp.int32, (slots, total), 0)
        for k, block in enumerate(blocks):
            first = block * per_out
            some = [
                jnp.where(keys[0, m : m + 1, :] == slot, 1.0, 0.0)
                for m in range(first, first + per_out)
            ]
            chosen[k] = jnp.concatenate(some).astype(chosen.dtype)

    tokens = rows[...].reshape(total, rows.shape[2])
    for k, out in enumerate(outs):
        found = jnp.dot(chosen[k], tokens, preferred_element_type=jnp.float32)
        out[...] = found.astype(out.dtype)


def picked(keys, gathered, section, lo, count, slots, size, blocks, part, parts):
    width = gathered.shape[2] // parts
    tile = width // 2 if width % 256 == 0 else width
    steps = width // tile
    total = lo * count
    per_out = keys.shape[1] // size
    shape = (per_out * slots, width)
    return pl.pallas_call(
        functools.partial(pick_kernel, slots, per_out, blocks),
        out_shape=[jax.ShapeDtypeStruct(shape, gathered.dtype)] * len(blocks),
        grid=(steps,),
        in_specs=[
            pl.BlockSpec((1, keys.shape[1], total), lambda i: (section, 0, 0)),
            pl.BlockSpec((lo, count, tile), lambda i: (section, 0, part * steps + i)),
        ],
        out_specs=[pl.BlockSpec((shape[0], tile), lambda i: (0, i))] * len(blocks),
        scratch_shapes=[pltpu.VMEM((len(blocks), shape[0], total), gathered.dtype)],
        name="picked",
    )(keys, gathered)


def row_kernel(at, rows, weight, out):
    found = lax.dot_general(
        rows[...], weight[...], (((1,), (1,)), ((), ())), preferred_element_type=jnp.float32
    )
    out[...] = found.astype(out.dtype)


def row_grad(at, rows, weight, block):
    width, half = weight.shape
    count = rows.shape[0] * rows.shape[1] // (2 * half)
    tile = 512 if width % 512 == 0 else width
    return pl.pallas_call(
        row_kernel,
        out_shape=jax.ShapeDtypeStruct((count, width), rows.dtype),
        grid_spec=pltpu.PrefetchScalarGridSpec(
            num_scalar_prefetch=1,
            grid=(width // tile,),
            in_specs=[
                pl.BlockSpec((count, half), block),
                pl.BlockSpec((tile, half), lambda i, at: (i, 0)),
            ],
            out_specs=pl.BlockSpec((count, tile), lambda i, at: (0, i)),
        ),
        name="row_grad",
    )(at, rows, weight)


def sum_kernel(slots, at, keys, rows, *refs):
    out, chosen = refs[-2], refs[-1]
    total = keys.shape[2]

    @pl.when(pl.program_id(0) == 0)
    def _():
        slot = lax.broadcasted_iota(jnp.int32, (slots, total), 0)
        some = [
            jnp.where(keys[0, m : m + 1, :] == slot, 1.0, 0.0) for m in range(keys.shape[1])
        ]
        chosen[...] = jnp.concatenate(some).T.astype(chosen.dtype)

    found = jnp.dot(chosen[...], rows[...], preferred_element_type=jnp.float32)
    out[...] = found.astype(out.dtype)


def token_sums(section, keys, rows, slots, before):
    count, width = rows.shape
    total = keys.shape[2]
    tile = width // 4 if width % 512 == 0 else width
    given = [] if before is None else [before]
    return pl.pallas_call(
        functools.partial(sum_kernel, slots),
        out_shape=jax.ShapeDtypeStruct((2 * total, width), rows.dtype),
        grid_spec=pltpu.PrefetchScalarGridSpec(
            num_scalar_prefetch=1,
            grid=(width // tile,),
            in_specs=[
                pl.BlockSpec((1, keys.shape[1], total), lambda i, at: (2 + at[0], 0, 0)),
                pl.BlockSpec((count, tile), lambda i, at: (0, i)),
            ]
            + [pl.BlockSpec(memory_space=pl.ANY)] * len(given),
            out_specs=pl.BlockSpec((total, tile), lambda i, at: (at[0], i)),
            scratch_shapes=[pltpu.VMEM((total, count), rows.dtype)],
        ),
        input_output_aliases={3: 0} if given else {},
        name="token_sums",
    )(section, keys, rows, *given)


def key_kernel(sizes, most, top, place, ids, out, named_all):
    _, _, n_x, n_lo, n_y = sizes
    plane, count = n_x * n_y, ids.shape[2]
    my_x, my_lo, my_y = place[0], place[1], place[2]
    member = lax.broadcasted_iota(jnp.int32, (plane, count), 0)
    major, minor = member // n_y, member % n_y
    orders = (
        (0, (my_x + major) % n_x, (my_y + minor) % n_y),
        (1, (my_x + minor) % n_x, (my_y + major) % n_y),
        (0, major, minor),
        (1, major, minor),
    )
    for i, (hi, at_x, at_y) in enumerate(orders):
        expert = ((at_x * n_lo + my_lo) * n_y + at_y).astype(jnp.float32)
        for lo in range(n_lo):
            some = ids[hi * n_lo + lo].astype(jnp.float32)
            named = expert == some[0:1]
            for k in range(1, top):
                named = named | (expert == some[k : k + 1])
            row = (i * n_lo + lo) * plane
            named_all[row : row + plane, :] = jnp.where(named, 1.0, 0.0)
    token = lax.broadcasted_iota(jnp.int32, (count, count), 0)
    later = lax.broadcasted_iota(jnp.int32, (count, count), 1)
    earlier = jnp.where(token < later, 1.0, 0.0).astype(jnp.bfloat16)
    before = jnp.dot(
        named_all[...].astype(jnp.bfloat16), earlier, preferred_element_type=jnp.float32
    )
    for i in range(len(orders)):
        for lo in range(n_lo):
            row = (i * n_lo + lo) * plane
            slot = before[row : row + plane].astype(jnp.int32) + lo * most
            key = jnp.where(named_all[row : row + plane, :] > 0.5, slot, -1)
            out[i, :, lo * count : (lo + 1) * count] = key


def key_table(sizes, most, top, count, place, gathered):
    _, _, n_x, n_lo, n_y = sizes
    rings, per_source, _ = gathered.shape
    spare = per_source - count
    shape = (4, n_x * n_y, n_lo * count)
    return pl.pallas_call(
        functools.partial(key_kernel, sizes, most, top),
        out_shape=jax.ShapeDtypeStruct(shape, jnp.int32),
        grid=(1,),
        in_specs=[
            pl.BlockSpec(memory_space=pltpu.SMEM),
            pl.BlockSpec((rings, spare, count), lambda i: (0, count // spare, 0)),
        ],
        out_specs=pl.BlockSpec(shape, lambda i: (0, 0, 0)),
        scratch_shapes=[pltpu.VMEM((4 * n_lo * n_x * n_y, count), jnp.float32)],
        name="key_table",
    )(place, gathered)


def on_device(sizes, tokens, expert_ids, up_weight, up_grad):
    n_hi, _, n_x, n_lo, n_y = sizes
    token_rows = tokens[0]
    count, width = token_rows.shape
    weight = up_weight[0, 0]
    half = weight.shape[1]
    sources, most = up_grad.shape[2], up_grad.shape[3]
    top = expert_ids.shape[2]
    rows = sources * most
    plane = n_x * n_y
    slots = n_lo * most
    low = lax.axis_index(HI) == 0
    rings = mirror_rings(sizes)
    ring_axes = (HI, CORE, LO)
    bf16 = jnp.bfloat16
    spare = 8

    grad = jnp.transpose(up_grad[0, 0], (1, 0, 2)).reshape(rows, 2 * half)
    place = jnp.arange(rows, dtype=jnp.int32)
    at_x, at_y = place // (n_y * slots), (place // slots) % n_y
    at_lo, at_slot = (place // most) % n_lo, place % most
    taken = at_slot * sources + (at_x * n_lo + at_lo) * n_y + at_y
    by_place = (taken[:, None] == place[None, :]).astype(bf16)
    grad = lax.optimization_barrier(dot(by_place, grad, ((1,), (0,))).astype(bf16))
    grad_send = jnp.where(low, grad[:, half:], grad[:, :half])
    pair = (HI, CORE)
    swapped = lax.all_gather(grad_send, pair, axis=0, axis_index_groups=mirror_pairs(sizes))

    id_rows = jnp.pad(expert_ids[0].T.astype(bf16), ((0, spare - top), (0, width - count)))
    outgoing = jnp.concatenate([token_rows, id_rows])
    gathered = lax.all_gather(outgoing, ring_axes, axis=0, axis_index_groups=rings, tiled=True)

    def exchange(value):
        value = value.reshape(plane, slots, width)
        return lax.all_to_all(value, (X, Y), 0, 0, tiled=True).reshape(rows, width)

    my_hi, my_x = lax.axis_index(HI), lax.axis_index(X)
    my_lo, my_y = lax.axis_index(LO), lax.axis_index(Y)
    my_hi = jnp.reshape(my_hi, (1,)).astype(jnp.int32)
    own_out = row_grad(my_hi, grad, weight, lambda i, at: (0, at[0]))
    own_out, my_hi, other, my_x, my_lo, my_y = lax.optimization_barrier(
        (own_out, my_hi, 1 - my_hi, my_x, my_lo, my_y)
    )
    own_back = exchange(own_out)
    own_back, swapped = lax.optimization_barrier((own_back, swapped))
    swapped = swapped.reshape(n_hi * rows, half)
    mirror_out = row_grad(other, swapped, weight, lambda i, at: (at[0], 0))
    mirror_back = exchange(mirror_out)
    own_back, mirror_back, grad, swapped, gathered = lax.optimization_barrier(
        (own_back, mirror_back, grad, swapped, gathered)
    )
    _, my_hi, other, my_x, my_lo, my_y, nil = lax.optimization_barrier(
        (mirror_back, my_hi, other, my_x, my_lo, my_y, jnp.int32(0))
    )
    grad_own = jnp.where(low, grad[:, :half], grad[:, half:])
    grad_mirror = jnp.where(low, swapped[rows:], swapped[:rows])

    gathered = gathered.reshape(n_hi * n_lo, count + spare, width)
    position = jnp.stack([my_x, my_lo, my_y]).astype(jnp.int32)
    keys = key_table(sizes, most, top, count, position, gathered)

    parts = 2
    routes = ((X, n_x, Y, n_y), (Y, n_y, X, n_x))
    near = {(part, section): [None] * n_x for part in range(parts) for section in range(n_hi)}
    turn = 0
    for part, blocks in ((0, (1, n_x - 1, 2, 0)), (1, (1, n_x - 1, 2, 0))):
        for section, (axis, size, _, _) in enumerate(routes):
            sent = picked(keys, gathered, section, n_lo, count, slots, size, blocks, part, parts)
            for block, value in zip(blocks, sent):
                near[part, section][block] = shifted(value, axis, size, block)
            turn += 1

    sums = token_sums(my_hi, keys, own_back, slots, None)
    sums = token_sums(other, keys, mirror_back, slots, sums)
    token_grad = lax.psum_scatter(
        sums, ring_axes, scatter_dimension=0, axis_index_groups=rings, tiled=True
    )

    far = {}
    for part in range(parts):
        for section, (_, _, axis, size) in enumerate(routes):
            turn = str(2 * part + section)
            turned = merged(near[part, section], slots)
            far[part, section] = [shifted(turned[i], axis, size, i) for i in range(size)]

    late = place + nil
    outer, inner, rest = late // (n_y * slots), (late // slots) % n_y, late % slots
    turned_grad = []
    for some, row_x, row_y in (
        (jnp.where(low, grad_own, grad_mirror), my_x - inner, my_y - outer),
        (jnp.where(low, grad_mirror, grad_own), my_x - outer, my_y - inner),
    ):
        row = ((row_x % n_x) * n_y + row_y % n_y) * slots + rest
        order = (row[:, None] == place[None, :]).astype(bf16)
        turned_grad.append(dot(order, some, ((1,), (0,))).astype(bf16))
    turned_grad = jnp.concatenate(turned_grad).reshape(n_y + n_x, -1, half)
    weight_grad = None
    for part in range(parts):
        pieces = far[part, 0] + far[part, 1]
        weight_grad = hidden_sum(turned_grad, pieces, part, parts, weight_grad)
    return (token_grad[None], weight_grad[None, None])


def solution(mesh):
    sizes = (2, 2, 4, 4, 4)
    fine = Mesh(mesh.devices.reshape(sizes), AXES)
    pipe, expert = (HI, CORE), (X, LO, Y)

    def device_body(*args):
        return on_device(sizes, *args)

    return jax.shard_map(
        device_body,
        mesh=fine,
        in_specs=(
            P(pipe, expert, None),
            P(pipe, expert, None),
            P(pipe, expert, None, None),
            P(pipe, expert, None, None, None),
        ),
        out_specs=(P(pipe, expert, None), P(pipe, expert, None, None)),
        check_vma=False,
    )
```
